128 devices in a mesh: row: 16 (over y_hi, z, core), col: 8 (over x, y_lo).
Axes of the slice: x: 4, y: 4 (y_hi: 2, y_lo: 2; y = y_hi * 2 + y_lo), z: 4, core: 2. Of those that a mesh axis runs over, the one named last changes fastest.
Arguments:
- factor: bfloat16 [16, 1536, 6144], P(None, 'row'), may hold values from -0.078125 to 0.078125
- inverse_blocks: bfloat16 [4, 1536, 1536], P(None, 'row'), as said below
- right_side: float32 [16, 1536, 4096], P(None, 'row', 'col'), may hold values from -6 to 6
- shape_derivative: float32 [4, 1536, 4096], P(None, 'row', 'col')
Outputs:
- solved: float32 [4, 1536, 4096], P(None, 'row', 'col')
- trailing: float32 [12, 1536, 4096], P(None, 'row', 'col')
- sensitivity: float32 [4, 1536], P(None, 'row')
The draws below stay inside these ranges and needn't reach their ends.
Inputs may be any that keep to these rules, and one draw needn't show every extreme that they name: inverse_blocks[k] is the inverse supplied for the diagonal block of step k.
All inputs are finite; a program needn't handle non-finite values.
Results may differ from the reference program's by a relative error of at most 0.0045.
Values may be sent and summed in bfloat16 or wider, within the bound.
No kernel may reach another device: no remote copies, remote signals or barrier semaphores. Data moves between devices by JAX's collectives and lax.ppermute only.
A program may use at most 128 MiB of HBM per device.

```python
import math
import jax
import jax.numpy as jnp
from jax import lax

NB = 1536
STEPS = 4
NBLK = 16
RHS = 4096
W = 6144


def draw_inverse_blocks(key, part):
    key_off = jax.random.fold_in(jax.random.fold_in(key, 11), 0)
    rough = jnp.clip(jax.random.normal(key_off, (STEPS, NB, NB), jnp.float32), -5.0, 5.0)
    diagonal_scale = jnp.ones((STEPS, NB, 1), jnp.float32)
    identity = (lax.broadcasted_iota(jnp.int32, (NB, NB), 0) == lax.broadcasted_iota(jnp.int32, (NB, NB), 1)).astype(jnp.float32)
    values = diagonal_scale * identity + 0.6 * rough / math.sqrt(NB)
    return values.astype(jnp.bfloat16)


def draw_shape_derivative(key, part):
    column = lax.broadcasted_iota(jnp.float32, (STEPS, NB, RHS), 2)
    key_val = jax.random.fold_in(key, 23)
    values = jnp.clip(jax.random.normal(key_val, (STEPS, NB, RHS), jnp.float32), -5.0, 5.0)
    ramp = 1.0 + 2.0 * column / (RHS - 1)
    return (values * ramp / math.sqrt(RHS)).astype(jnp.float32)


def block_scale(rng, dims, pieces, least, largest):
    loudness = 1.0
    for position, shards_of in pieces:
        heights = jax.random.uniform(jax.random.fold_in(jax.random.fold_in(rng, 6), position), (shards_of,), jnp.float32, least / len(pieces), largest / len(pieces))
        loudness = loudness * jnp.repeat(jnp.exp(heights), dims[position] // shards_of).reshape((-1,) + (1,) * (len(dims) - 1 - position))
    return loudness


def noise(key, shape, scale, limit, shards=(), kind=jnp.bfloat16):
    result = scale * jax.random.normal(key, shape, jnp.float32)
    if shards:
        result = result * block_scale(key, shape, shards, -0.22, 0.18)
    return jnp.clip(result, -limit, limit).astype(kind)


def setup_inputs(seed: int = 0) -> dict:
    key_of = jax.random.split(jax.random.key(seed), 5)
    factor = noise(key_of[0], (NBLK, NB, W), W ** -0.5, 0.078125, ((1, 16),))
    inverse_blocks = draw_inverse_blocks(jax.random.fold_in(key_of[4], 71), 0)
    right_side = noise(key_of[2], (NBLK, NB, RHS), 1.0, 6.0, ((1, 16), (2, 8)), jnp.float32)
    shape_derivative = draw_shape_derivative(jax.random.fold_in(key_of[4], 71), 0)
    return dict(factor=factor, inverse_blocks=inverse_blocks, right_side=right_side, shape_derivative=shape_derivative)


def reference(factor, inverse_blocks, right_side, shape_derivative):
    solved_list = []
    rounded_list = []
    for step in range(STEPS):
        residual = right_side[step]
        for earlier in range(step):
            panel = factor[step, :, earlier * NB:(earlier + 1) * NB]
            residual = residual - jnp.dot(panel, rounded_list[earlier], preferred_element_type=jnp.float32)
        residual_block = residual.astype(jnp.bfloat16)
        solution = jnp.dot(inverse_blocks[step], residual_block, preferred_element_type=jnp.float32)
        solved_list.append(solution)
        rounded_list.append(solution.astype(jnp.bfloat16))
    all_solved = jnp.concatenate(rounded_list, axis=0)
    trailing_list = []
    for block_row in range(STEPS, NBLK):
        product = jnp.dot(factor[block_row], all_solved, preferred_element_type=jnp.float32)
        trailing_list.append(right_side[block_row] - product)
    solved = jnp.stack(solved_list)
    trailing = jnp.stack(trailing_list)
    sensitivity = jnp.sum(solved * shape_derivative, axis=2)
    return solved, trailing, sensitivity
```

```python
import functools

import jax
import jax.numpy as jnp
from jax import lax
from jax.experimental import pallas as pl
from jax.experimental.pallas import tpu as pltpu
from jax.sharding import PartitionSpec as P

BF, F32 = jnp.bfloat16, jnp.float32


def perm(fn):
    out = []
    for i in range(16):
        y, z, c = fn(i // 8, (i // 2) % 4, i % 2)
        out.append((i, (y % 2) * 8 + (z % 4) * 2 + c % 2))
    return out


TO_Y = perm(lambda y, z, c: (y + 1, z, c))
TO_C = perm(lambda y, z, c: (y, z, c + 1))
Z_A = perm(lambda y, z, c: (y, z + 1 - 2 * c, c))
Z_B = perm(lambda y, z, c: (y, z - 1 + 2 * c, c))
Z_D = perm(lambda y, z, c: (y, z + 2, c))


def pp(x, pairs):
    return lax.ppermute(x, "row", pairs)


def place():
    i = lax.axis_index("row")
    return i // 8, (i // 2) % 4, i % 2


def z_gather(shard):
    return [shard, pp(shard, Z_A), pp(shard, Z_B), pp(shard, Z_D)]


def assemble(shards, full):
    y, z, c = place()
    step = 2 * c - 1
    for ref, off in zip(shards, (0, step, -step, 2)):
        zz = lax.rem(z + off + 4, 4)
        for yy in range(2):
            for cc in range(2):
                full[yy, zz, cc * 96 : (cc + 1) * 96, :] = ref[2 * yy + cc]


def matmul4(pieces, full):
    lhs = jnp.concatenate([p[...] for p in pieces], axis=0)
    return jnp.dot(lhs, full[...].reshape(-1, 128), preferred_element_type=F32)


def store4(out, product, base=None):
    y, z, c = place()
    for rel in range(4):
        q = lax.rem(y + rel // 2, 2) * 2 + lax.rem(c + rel % 2, 2)
        value = product[rel * 96 : (rel + 1) * 96]
        if base is not None:
            value = base[q] - value
        out[q] = value.astype(out.dtype)


def solve_kernel(t0, t1, t2, t3, a0, a1, a2, a3, out, full):
    assemble((t0, t1, t2, t3), full)
    store4(out, matmul4((a0, a1, a2, a3), full))


def update_kernel(s0, s1, s2, s3, a0, a1, a2, a3, acc, out, full):
    assemble((s0, s1, s2, s3), full)
    store4(out, matmul4((a0, a1, a2, a3), full), acc)


def late_kernel(full, a0, a1, a2, a3, acc, out):
    store4(out, matmul4((a0, a1, a2, a3), full), acc)


def collect_kernel(s0, s1, s2, s3, full):
    assemble((s0, s1, s2, s3), full)


FULL = (2, 4, 192, 128)


def whole(shape):
    return pl.BlockSpec(shape, lambda i: (0,) * len(shape))


SHARD = whole((4, 96, 128))


def piece_specs(own, own_index, col):
    own_spec = pl.BlockSpec((None, 96, 1536), lambda i: own_index)
    return [
        own_spec,
        pl.BlockSpec((None, 96, 1536), lambda i: (0, 0, col)),
        pl.BlockSpec((96, 1536), lambda i: (0, col)),
        pl.BlockSpec((None, 96, 1536), lambda i: (1, 0, col)),
    ]


COST = pl.CostEstimate(flops=2 * 384 * 1536 * 128, transcendentals=0, bytes_accessed=1600000)


def solve(shards, own, own_index, swapped, recv, col):
    return pl.pallas_call(
        solve_kernel,
        grid=(1,),
        in_specs=[SHARD] * 4 + piece_specs(own, own_index, col),
        out_specs=SHARD,
        out_shape=jax.ShapeDtypeStruct((4, 96, 128), BF),
        scratch_shapes=[pltpu.VMEM(FULL, BF)],
        cost_estimate=COST,
        name="solve",
    )(*shards, own, swapped, recv, swapped)


def update(shards, own, own_index, swapped, recv, col, acc):
    return pl.pallas_call(
        update_kernel,
        grid=(1,),
        in_specs=[SHARD] * 4 + piece_specs(own, own_index, col) + [SHARD],
        out_specs=(SHARD, whole(FULL)),
        out_shape=(jax.ShapeDtypeStruct((4, 96, 128), BF), jax.ShapeDtypeStruct(FULL, BF)),
        cost_estimate=COST,
        name="update",
    )(*shards, own, swapped, recv, swapped, acc)


def late(full, own, own_index, swapped, recv, col, acc):
    return pl.pallas_call(
        late_kernel,
        grid=(1,),
        in_specs=[whole(FULL)] + piece_specs(own, own_index, col) + [SHARD],
        out_specs=SHARD,
        out_shape=jax.ShapeDtypeStruct((4, 96, 128), F32),
        cost_estimate=COST,
        name="late",
    )(full, own, swapped, recv, swapped, acc)


def collect(shards):
    return pl.pallas_call(
        collect_kernel,
        grid=(1,),
        in_specs=[SHARD] * 4,
        out_specs=whole(FULL),
        out_shape=jax.ShapeDtypeStruct(FULL, BF),
        name="collect",
    )(*shards)


def trail_kernel(k, s_own, s_y, s_c, s_yc, fac, acc, deriv, *rest):
    out, solved, sens, full = rest[-4:]
    y, z, c = place()

    @pl.when(pl.program_id(0) == 0)
    def _():
        for rel, ref in enumerate((s_own, s_c, s_y, s_yc)):
            q = lax.rem(y + rel // 2, 2) * 2 + lax.rem(c + rel % 2, 2)
            full[:, pl.ds(pl.multiple_of(q * 128, 128), 128)] = ref[...]
        rows = full[pl.ds(pl.multiple_of((y * 8 + z * 2 + c) * 96, 32), 96), :].astype(F32)
        solved[...] = rows
        terms = rows * deriv[...]
        sens[...] = (terms[:, :128] + terms[:, 128:256]) + (terms[:, 256:384] + terms[:, 384:])

    lhs = fac[...].reshape(-1, 1536)
    out[...] = acc[...] - jnp.dot(lhs, full[...], preferred_element_type=F32).reshape(out.shape)


def trail(k, s_own, s_y, s_swap, factor, acc, deriv, solved):
    first = k == 0
    cols = pl.BlockSpec((1536, 128), lambda i: (0, 0))
    aliases = {5: 0} if not first else {}
    in_specs = [
        cols,
        cols,
        pl.BlockSpec((None, 1536, 128), lambda i: (0, 0, 0)),
        pl.BlockSpec((None, 1536, 128), lambda i: (1, 0, 0)),
        pl.BlockSpec((4, 96, 1536), lambda i: (i + 1, 0, k)),
        pl.BlockSpec((4, 96, 512), (lambda i: (i + 1, 0, 0)) if first else (lambda i: (i, 0, 0))),
        pl.BlockSpec((None, 96, 512), lambda i: (k, 0, 0)),
    ]
    args = [s_own, s_y, s_swap, s_swap, factor, acc, deriv]
    if not first:
        in_specs.append(pl.BlockSpec(memory_space=pl.ANY))
        args.append(solved)
        aliases[7] = 1
    return pl.pallas_call(
        functools.partial(trail_kernel, k),
        grid=(3,),
        in_specs=in_specs,
        out_specs=(
            pl.BlockSpec((4, 96, 512), lambda i: (i, 0, 0)),
            pl.BlockSpec((None, 96, 512), lambda i: (k, 0, 0)),
            pl.BlockSpec((96, 128), lambda i: (0, 0)),
        ),
        out_shape=(
            jax.ShapeDtypeStruct((12, 96, 512), F32),
            jax.ShapeDtypeStruct((4, 96, 512), F32),
            jax.ShapeDtypeStruct((96, 128), F32),
        ),
        scratch_shapes=[pltpu.VMEM((1536, 512), BF)],
        input_output_aliases=aliases,
        cost_estimate=pl.CostEstimate(flops=2 * 1152 * 1536 * 512, transcendentals=0, bytes_accessed=9000000),
        name="trail",
    )(*args)


def cut(x, start, size):
    return lax.dynamic_slice_in_dim(x, start, size, axis=x.ndim - 1)


def ordered(pieces):
    y, z, c = place()
    own, sib, yp, yps = pieces
    low = [jnp.where(c == 0, own, sib), jnp.where(c == 0, sib, own)]
    high = [jnp.where(c == 0, yp, yps), jnp.where(c == 0, yps, yp)]
    first = [jnp.where(y == 0, a, b) for a, b in zip(low, high)]
    second = [jnp.where(y == 0, b, a) for a, b in zip(low, high)]
    return jnp.stack(first + second)


def spread_rows(own):
    y, z, c = place()
    to_y = cut(own, (1 - y) * 256, 256)
    keep = cut(own, y * 256, 256)
    from_y = pp(to_y, TO_Y)
    send = jnp.stack([cut(keep, (1 - c) * 128, 128), cut(from_y, (1 - c) * 128, 128)])
    got = pp(send, TO_C)
    return cut(keep, c * 128, 128), got[0], cut(from_y, c * 128, 128), got[1]


def local(factor, inverse_blocks, right_side, shape_derivative):
    pieces = spread_rows(right_side[0].astype(BF))
    t = ordered(pieces)
    sets = []
    for j in range(4):
        own = inverse_blocks[j]
        if j:
            own = jnp.concatenate([factor[j, :, : j * 1536], own], axis=1)
        recv = pp(own, TO_Y)
        swapped = pp(jnp.stack([own, recv]), TO_C)
        sets.append((swapped, recv))
    rest = right_side[1:4]
    high = rest.astype(BF)
    low = (rest - high.astype(F32)).astype(BF)
    split = spread_rows(jnp.concatenate([high, low], axis=0))
    sums = ordered([p[:3].astype(F32) + p[3:].astype(F32) for p in split])
    accs = [None] + [sums[:, j] for j in range(3)]

    acc, solved, sens = right_side, None, []
    for k in range(4):
        shards = z_gather(t)
        s = solve(shards, inverse_blocks, (k, 0, 0), *sets[k], k)
        shards = z_gather(s)
        if k < 3:
            t, full = update(shards, factor, (k + 1, 0, k), *sets[k + 1], k, accs[k + 1])
            for j in range(k + 2, 4):
                accs[j] = late(full, factor, (j, 0, k), *sets[j], k, accs[j])
        else:
            full = collect(shards)
        s_own = full.reshape(1536, 128)
        s_y = pp(s_own, TO_Y)
        s_swap = pp(jnp.stack([s_own, s_y]), TO_C)
        acc, solved, part = trail(k, s_own, s_y, s_swap, factor, acc, shape_derivative, solved)
        sens.append(part)
    total = jnp.sum(jnp.stack(sens), axis=2)
    for mask in (1, 2, 6):
        total = total + lax.ppermute(total, "col", [(i, i ^ mask) for i in range(8)])
    return solved, acc, total


def solution(mesh):
    placed = (
        P(None, "row", None),
        P(None, "row", None),
        P(None, "row", "col"),
        P(None, "row", "col"),
    )
    return jax.shard_map(
        local,
        mesh=mesh,
        in_specs=placed,
        out_specs=(P(None, "row", "col"), P(None, "row", "col"), P(None, "row")),
        check_vma=False,
    )
```

```python
import functools

import jax
import jax.numpy as jnp
from jax import lax
from jax.experimental import pallas as pl
from jax.experimental.pallas import tpu as pltpu
from jax.sharding import PartitionSpec as P


BF, F32 = jnp.bfloat16, jnp.float32


def perm(fn):
    out = []
    for i in range(16):
        y, z, c = fn(i // 8, (i // 2) % 4, i % 2)
        out.append((i, (y % 2) * 8 + (z % 4) * 2 + c % 2))
    return out


TO_Y = perm(lambda y, z, c: (y + 1, z, c))
TO_C = perm(lambda y, z, c: (y, z, c + 1))
Z_A = perm(lambda y, z, c: (y, z + 1 - 2 * c, c))
Z_B = perm(lambda y, z, c: (y, z - 1 + 2 * c, c))
Z_D = perm(lambda y, z, c: (y, z + 2, c))


def pp(x, pairs):
    return lax.ppermute(x, "row", pairs)


def place():
    i = lax.axis_index("row")
    return i // 8, (i // 2) % 4, i % 2


def z_gather(shard):
    return [shard] + [pp(shard, pairs) for pairs in (Z_A, Z_B, Z_D)]


def assemble(shards, full):
    _, z, c = place()
    step = 2 * c - 1
    for ref, off in zip(shards, (0, step, -step, 2)):
        zz = lax.rem(z + off + 4, 4)
        for yy in range(2):
            for cc in range(2):
                full[yy, zz, cc * 96 : (cc + 1) * 96, :] = ref[2 * yy + cc]


def matmul4(pieces, full):
    lhs = jnp.concatenate([p[...] for p in pieces], axis=0)
    return jnp.dot(lhs, full[...].reshape(-1, 128), preferred_element_type=F32)


def store4(out, product, base=None):
    y, _, c = place()
    for rel in range(4):
        q = lax.rem(y + rel // 2, 2) * 2 + lax.rem(c + rel % 2, 2)
        value = product[rel * 96 : (rel + 1) * 96]
        if base is not None:
            value = base[q] - value
        out[q] = value.astype(out.dtype)


def x_odd():
    return lax.rem(lax.axis_index("col") // 2, 2)


def pack_kernel(j, halves, fac, inv, rows, own, *rest):
    y, _, _ = place()
    width = (j + 1) * 1536
    own[:, : j * 1536] = fac[...]
    own[:, j * 1536 : width] = inv[...]
    send, base = own, width
    if halves:
        send, base = rest[0], width // 2
        send[:, :base] = own[:, pl.ds(pl.multiple_of(x_odd() * base, 128), base)]
    n = rows.shape[0] if rows is not None else 0
    for m in range(n):
        value = rows[m, :, pl.ds(pl.multiple_of((1 - y) * 256, 128), 256)]
        high = value.astype(BF)
        send[:, base + m * 256 : base + (m + 1) * 256] = high
        send[:, base + (n + m) * 256 : base + (n + m + 1) * 256] = (value - high.astype(F32)).astype(BF)


def pack(j, halves, n, factor, inverse_blocks, right_side):
    width = (j + 1) * 1536
    extra = n * 512
    shapes = [(96, width), (96, width // 2 + extra)] if halves else [(96, width + extra)]
    in_specs = [
        pl.BlockSpec((None, 96, j * 1536), lambda i: (j, 0, 0)),
        pl.BlockSpec((None, 96, 1536), lambda i: (j, 0, 0)),
    ]
    args = [factor, inverse_blocks]
    kernel = functools.partial(pack_kernel, j, halves)
    if n:
        in_specs.append(pl.BlockSpec((n, 96, 512), lambda i: (j // n, 0, 0)))
        args.append(right_side)
    else:
        kernel = lambda fac, inv, *outs: pack_kernel(j, halves, fac, inv, None, *outs)
    return pl.pallas_call(
        kernel,
        grid=(1,),
        in_specs=in_specs,
        out_specs=[whole(x) for x in shapes],
        out_shape=[jax.ShapeDtypeStruct(x, BF) for x in shapes],
        cost_estimate=COST,
        compiler_params=grant(10),
        name="pack",
    )(*args)


def solve_kernel(t0, t1, t2, t3, a0, a1, a2, a3, out, kept, full):
    assemble((t0, t1, t2, t3), full)
    product = matmul4((a0, a1, a2, a3), full)
    store4(out, product)
    store4(kept, product)


def update_kernel(s0, s1, s2, s3, a0, a1, a2, a3, acc, out, full):
    assemble((s0, s1, s2, s3), full)
    store4(out, matmul4((a0, a1, a2, a3), full), acc)


def late_kernel(full, a0, a1, a2, a3, acc, out):
    store4(out, matmul4((a0, a1, a2, a3), full), acc)


def collect_kernel(s0, s1, s2, s3, full):
    assemble((s0, s1, s2, s3), full)


FULL = (2, 4, 192, 128)


def whole(shape):
    return pl.BlockSpec(shape, lambda i: (0,) * len(shape))


SHARD = whole((4, 96, 128))


def piece_specs(col):
    return [pl.BlockSpec((96, 1536), lambda i: (0, col))] * 4


def grant(mib):
    return pltpu.CompilerParams(vmem_limit_bytes=mib << 20)


COST = pl.CostEstimate(flops=2 * 384 * 1536 * 128, transcendentals=0, bytes_accessed=1600000)


def solve(shards, pieces, col):
    return pl.pallas_call(
        solve_kernel,
        grid=(1,),
        in_specs=[SHARD] * 4 + piece_specs(col),
        out_specs=(SHARD, SHARD),
        out_shape=(jax.ShapeDtypeStruct((4, 96, 128), BF), jax.ShapeDtypeStruct((4, 96, 128), F32)),
        scratch_shapes=[pltpu.VMEM(FULL, BF)],
        cost_estimate=COST,
        compiler_params=grant(6),
        name="solve",
    )(*shards, *pieces)


def update(shards, pieces, col, acc):
    return pl.pallas_call(
        update_kernel,
        grid=(1,),
        in_specs=[SHARD] * 4 + piece_specs(col) + [SHARD],
        out_specs=(SHARD, whole(FULL)),
        out_shape=(jax.ShapeDtypeStruct((4, 96, 128), BF), jax.ShapeDtypeStruct(FULL, BF)),
        cost_estimate=COST,
        compiler_params=grant(6),
        name="update",
    )(*shards, *pieces, acc)


def late(full, pieces, col, acc):
    return pl.pallas_call(
        late_kernel,
        grid=(1,),
        in_specs=[whole(FULL)] + piece_specs(col) + [SHARD],
        out_specs=SHARD,
        out_shape=jax.ShapeDtypeStruct((4, 96, 128), F32),
        cost_estimate=COST,
        compiler_params=grant(6),
        name="late",
    )(full, *pieces, acc)


def collect(shards):
    return pl.pallas_call(
        collect_kernel,
        grid=(1,),
        in_specs=[SHARD] * 4,
        out_specs=whole(FULL),
        out_shape=jax.ShapeDtypeStruct(FULL, BF),
        compiler_params=grant(4),
        name="collect",
    )(*shards)


def trail_kernel(s_own, s_c, s_y, s_yc, fac, acc, *rest):
    out, solved = rest[-2:]
    y, z, c = place()
    columns = (s_own, s_c, s_y, s_yc)

    def spot(rel):
        q = lax.rem(y + rel // 2, 2) * 2 + lax.rem(c + rel % 2, 2)
        return pl.ds(pl.multiple_of(q * 128, 128), 128)

    @pl.when(pl.program_id(0) == 0)
    def _():
        rows = pl.ds(pl.multiple_of((y * 8 + z * 2 + c) * 96, 32), 96)
        for rel, ref in enumerate(columns):
            solved[:, spot(rel)] = ref[rows, :].astype(F32)

    lhs = fac[...].reshape(-1, 1536)
    rhs = jnp.concatenate([ref[...] for ref in columns], axis=1)
    product = jnp.dot(lhs, rhs, preferred_element_type=F32).reshape(-1, 96, 512)
    for rel in range(4):
        out[:, :, spot(rel)] = acc[:, :, spot(rel)] - product[:, :, rel * 128 : (rel + 1) * 128]


def trail(k, columns, factor, acc, solved):
    first = k == 0
    cols = pl.BlockSpec((1536, 128), lambda i: (0, 0))
    aliases = {5: 0} if not first else {}
    in_specs = [
        cols,
        cols,
        cols,
        cols,
        pl.BlockSpec((4, 96, 1536), lambda i: (i + 1, 0, k)),
        pl.BlockSpec((4, 96, 512), (lambda i: (i + 1, 0, 0)) if first else (lambda i: (i, 0, 0))),
    ]
    args = [*columns, factor, acc]
    if not first:
        in_specs.append(pl.BlockSpec(memory_space=pl.ANY))
        args.append(solved)
        aliases[6] = 1
    return pl.pallas_call(
        trail_kernel,
        grid=(3,),
        in_specs=in_specs,
        out_specs=(
            pl.BlockSpec((4, 96, 512), lambda i: (i, 0, 0)),
            pl.BlockSpec((None, 96, 512), lambda i: (k, 0, 0)),
        ),
        out_shape=(
            jax.ShapeDtypeStruct((12, 96, 512), F32),
            jax.ShapeDtypeStruct((4, 96, 512), F32),
        ),
        input_output_aliases=aliases,
        cost_estimate=pl.CostEstimate(flops=2 * 1152 * 1536 * 512, transcendentals=0, bytes_accessed=9000000),
        compiler_params=grant(14),
        name="trail",
    )(*args)


def cut(x, start, size):
    return lax.dynamic_slice_in_dim(x, start, size, axis=x.ndim - 1)


def ordered(pieces):
    y, _, c = place()
    own, sib, yp, yps = pieces
    low = [jnp.where(c == 0, own, sib), jnp.where(c == 0, sib, own)]
    high = [jnp.where(c == 0, yp, yps), jnp.where(c == 0, yps, yp)]
    first = [jnp.where(y == 0, a, b) for a, b in zip(low, high)]
    second = [jnp.where(y == 0, b, a) for a, b in zip(low, high)]
    return jnp.stack(first + second)


def after(x, *values):
    return lax.optimization_barrier((x, *values))[0]


def to_partner(own):
    y, _, _ = place()
    return cut(own, (1 - y) * 256, 256)


def land(own, from_y):
    y, _, c = place()
    keep = cut(own, y * 256, 256)
    send = jnp.stack([cut(keep, (1 - c) * 128, 128), cut(from_y, (1 - c) * 128, 128)])
    got = pp(send, TO_C)
    return cut(keep, c * 128, 128), got[0], cut(from_y, c * 128, 128), got[1]


def spread_rows(own, hold):
    from_y = pp(to_partner(own), TO_Y)
    return land(own, from_y if hold is None else after(from_y, hold))


def two_parts(x):
    high = x.astype(BF)
    return jnp.concatenate([high, (x - high.astype(F32)).astype(BF)], axis=0)


def joined(pieces):
    n = pieces[0].shape[0] // 2
    return ordered([p[:n].astype(F32) + p[n:].astype(F32) for p in pieces])


def apart(x, n):
    w = x.shape[1] // n
    return jnp.stack([x[:, j * w : (j + 1) * w] for j in range(n)])


def rows_of(own):
    sib = pp(own, TO_C)
    recv = pp(own, TO_Y)
    return own, sib, recv, pp(recv, TO_C)


def swap_halves(mine):
    return lax.ppermute(mine, "col", [(i, i ^ 2) for i in range(8)])


def rows_by_halves(own, mine, other):
    sib = pp(own, TO_C)
    odd = x_odd()
    recv = jnp.where(odd == 0, jnp.concatenate([mine, other], axis=1), jnp.concatenate([other, mine], axis=1))
    return own, sib, recv, pp(recv, TO_C)


def steps(factor, inverse_blocks, right_side, shape_derivative):
    factor, inverse_hbm, right_hbm = (
        pltpu.with_memory_space_constraint(x, pltpu.HBM) for x in (factor, inverse_blocks, right_side)
    )
    t = ordered(spread_rows(right_side[0].astype(BF)[None], None))[:, 0]

    sets = [rows_of(inverse_blocks[0])]
    rows1 = two_parts(right_side[1:2])
    sets.append(rows_of(pack(1, False, 1, factor, inverse_hbm, right_hbm)[0]))
    first = joined(land(rows1, apart(sets[1][2][:, 3072:], 2)))[:, 0]
    accs = [None, first, None, None]
    own2, mine2 = pack(2, True, 2, factor, inverse_hbm, right_hbm)
    rows23 = two_parts(after(right_side, t)[2:4])
    mine2 = pp(mine2, TO_Y)
    own3, mine3 = pack(3, True, 0, factor, inverse_hbm, right_hbm)
    mine3 = pp(mine3, TO_Y)

    acc, solved, columns, fulls, kept = right_hbm, None, [], [], []

    def trail_step(k, acc, solved):
        return trail(k, columns[k], factor, acc, solved)

    def late_step(j, m):
        accs[j] = late(fulls[m], sets[j], m, accs[j])

    for k in range(4):
        shards = z_gather(t)
        if k == 3:
            acc, solved = trail_step(1, acc, solved)
        if k == 2:
            sets.append(rows_by_halves(own3, mine3, after(other3, t)))
            late_step(3, 0)
            late_step(3, 1)
        s, product = solve(shards, sets[k], k)
        kept.append(product)
        shards = z_gather(s)
        if k == 2:
            acc, solved = trail_step(0, acc, solved)
        if k < 3:
            t, full = update(shards, sets[k + 1], k, accs[k + 1])
            fulls.append(full)
            if k == 0:
                mine2 = after(mine2, t)
                later = joined(land(rows23, apart(mine2[:, 2304:], 4)))
                accs[2:] = later[:, 0], later[:, 1]
                mine2 = mine2[:, :2304]
                sets.append(rows_by_halves(own2, mine2, swap_halves(mine2)))
                late_step(2, 0)
            if k == 1:
                other3 = swap_halves(mine3)
                held = after(shape_derivative, s)
            if k == 2:
                deriv = ordered(spread_rows(held, t))
        else:
            full = collect(shards)
        s_own = full.reshape(1536, 128)
        s_y = pp(s_own, TO_Y)
        columns.append((s_own, pp(s_own, TO_C), s_y, pp(s_y, TO_C)))
    acc, solved = trail_step(2, acc, solved)
    total = jnp.sum(jnp.stack(kept, axis=1) * deriv, axis=3)
    total = total + pp(total, TO_C)
    total = total + lax.ppermute(total, "col", [(i, i ^ 1) for i in range(8)])
    total = total + lax.ppermute(total, ("row", "col"), [(i, i ^ 65) for i in range(128)])
    for mask in (2, 6):
        total = total + lax.ppermute(total, "col", [(i, i ^ mask) for i in range(8)])
    acc, solved = trail_step(3, acc, solved)
    y, _, c = place()
    return solved, acc, lax.dynamic_index_in_dim(total, y * 2 + c, axis=0, keepdims=False)


def solution(mesh):
    placed = (
        P(None, "row", None),
        P(None, "row", None),
        P(None, "row", "col"),
        P(None, "row", "col"),
    )
    return jax.shard_map(
        steps,
        mesh=mesh,
        in_specs=placed,
        out_specs=(P(None, "row", "col"), P(None, "row", "col"), P(None, "row")),
        check_vma=False,
    )
```

```python
import functools

import jax
import jax.numpy as jnp
from jax import lax
from jax.experimental import pallas as pl
from jax.experimental.pallas import tpu as pltpu
from jax.sharding import PartitionSpec as P


BF, F32 = jnp.bfloat16, jnp.float32


def perm(fn):
    out = []
    for i in range(16):
        y, z, c = fn(i // 8, (i // 2) % 4, i % 2)
        out.append((i, (y % 2) * 8 + (z % 4) * 2 + c % 2))
    return out


TO_Y = perm(lambda y, z, c: (y + 1, z, c))
TO_C = perm(lambda y, z, c: (y, z, c + 1))
Z_A = perm(lambda y, z, c: (y, z + 1 - 2 * c, c))
Z_B = perm(lambda y, z, c: (y, z - 1 + 2 * c, c))
Z_D = perm(lambda y, z, c: (y, z + 2, c))


def pp(x, pairs):
    return lax.ppermute(x, "row", pairs)


def place():
    i = lax.axis_index("row")
    return i // 8, (i // 2) % 4, i % 2


def z_gather(shard):
    return [shard] + [pp(shard, pairs) for pairs in (Z_A, Z_B, Z_D)]


def assemble(shards, full):
    _, z, c = place()
    step = 2 * c - 1
    for ref, off in zip(shards, (0, step, -step, 2)):
        zz = lax.rem(z + off + 4, 4)
        for yy in range(2):
            for cc in range(2):
                full[yy, zz, cc * 96 : (cc + 1) * 96, :] = ref[2 * yy + cc]


def matmul4(pieces, full):
    lhs = jnp.concatenate([p[...] for p in pieces], axis=0)
    return jnp.dot(lhs, full[...].reshape(-1, 128), preferred_element_type=F32)


def store4(out, product, base=None):
    y, _, c = place()
    for rel in range(4):
        q = lax.rem(y + rel // 2, 2) * 2 + lax.rem(c + rel % 2, 2)
        value = product[rel * 96 : (rel + 1) * 96]
        if base is not None:
            value = base[q] - value
        out[q] = value.astype(out.dtype)


def x_odd():
    return lax.rem(lax.axis_index("col") // 2, 2)


def lanes(start, size=128):
    return pl.ds(pl.multiple_of(start, 128), size)


def local_call(kernel, args, specs, shapes, mib=10):
    return pl.pallas_call(
        kernel,
        grid=(1,),
        in_specs=specs,
        out_specs=[whole(x.shape) for x in shapes],
        out_shape=shapes,
        cost_estimate=COST,
        compiler_params=grant(mib),
    )(*args)


def pack_kernel(j, halves, n, fac, inv, *refs):
    y, _, _ = place()
    outs = list(refs[1:] if n else refs)
    width = (j + 1) * 1536
    own = outs.pop(0)
    own[:, : j * 1536] = fac[...]
    own[:, j * 1536 : width] = inv[...]
    if halves:
        outs.pop(0)[...] = own[:, lanes(x_odd() * (width // 2), width // 2)]
    for m in range(n):
        for out, half in zip(outs, (1 - y, y)):
            value = refs[0][m, :, lanes(half * 256, 256)]
            high = value.astype(BF)
            out[m] = high
            out[n + m] = (value - high.astype(F32)).astype(BF)


def pack(j, halves, n, factor, inverse_blocks, right_side):
    width = (j + 1) * 1536
    shapes = [(96, width)] + [(96, width // 2)] * halves + [(2 * n, 96, 256)] * (2 if n else 0)
    specs = [
        pl.BlockSpec((None, 96, j * 1536), lambda i: (j, 0, 0)),
        pl.BlockSpec((None, 96, 1536), lambda i: (j, 0, 0)),
    ] + ([pl.BlockSpec((n, 96, 512), lambda i: (j // n, 0, 0))] if n else [])
    args = [factor, inverse_blocks] + [right_side] * (n > 0)
    kernel = functools.partial(pack_kernel, j, halves, n)
    return local_call(kernel, args, specs, [jax.ShapeDtypeStruct(x, BF) for x in shapes])


def divide_kernel(rows, to_y, keep):
    y, _, _ = place()
    for out, half in ((to_y, 1 - y), (keep, y)):
        out[0] = rows[:, lanes(half * 256, 256)].astype(out.dtype)


def divide(x, k, kind):
    spec = pl.BlockSpec((None, 96, 512), lambda i: (k, 0, 0))
    return local_call(divide_kernel, [x], [spec], [jax.ShapeDtypeStruct((1, 96, 256), kind)] * 2)


def send_kernel(keep, from_y, send):
    _, _, c = place()
    for j in range(keep.shape[0]):
        send[0, j] = keep[j, :, lanes((1 - c) * 128)]
        send[1, j] = from_y[j, :, lanes((1 - c) * 128)]


def land_kernel(n, keep, from_y, got, out):
    y, _, c = place()
    m = keep.shape[0]
    for j in range(n):
        for rel in range(4):
            ref = from_y if rel // 2 else keep

            def piece(i):
                return got[rel // 2, i] if rel % 2 else ref[i, :, lanes(c * 128)]

            value = piece(j)
            if m > n:
                value = value.astype(F32) + piece(n + j).astype(F32)
            out[j, lax.rem(y + rel // 2, 2) * 2 + lax.rem(c + rel % 2, 2)] = value


def land(keep, from_y, n):
    m, kind = keep.shape[0], keep.dtype
    halves, quarters = whole((m, 96, 256)), whole((2, m, 96, 128))
    send = local_call(send_kernel, [keep, from_y], [halves] * 2, [jax.ShapeDtypeStruct((2, m, 96, 128), kind)])[0]
    got = pp(send, TO_C)
    out = jax.ShapeDtypeStruct((n, 4, 96, 128), F32 if m > n else kind)
    return local_call(functools.partial(land_kernel, n), [keep, from_y, got], [halves, halves, quarters], [out])[0]


def pick_kernel(total, out):
    y, _, c = place()
    row = total[:, 0, :]
    for q in range(1, 4):
        row = jnp.where(y * 2 + c == q, total[:, q, :], row)
    out[...] = row


def merge_kernel(mine, other, recv):
    half = mine.shape[1]
    recv[:, lanes(x_odd() * half, half)] = mine[...]
    recv[:, lanes((1 - x_odd()) * half, half)] = other[...]


def merge(mine, other):
    out = jax.ShapeDtypeStruct((96, 2 * mine.shape[1]), BF)
    return local_call(merge_kernel, [mine, other], [whole(mine.shape)] * 2, [out])[0]


def solve_kernel(t0, t1, t2, t3, a0, a1, a2, a3, out, kept, full):
    assemble((t0, t1, t2, t3), full)
    product = matmul4((a0, a1, a2, a3), full)
    store4(out, product)
    store4(kept, product)


def update_kernel(s0, s1, s2, s3, a0, a1, a2, a3, acc, out, full):
    assemble((s0, s1, s2, s3), full)
    store4(out, matmul4((a0, a1, a2, a3), full), acc)


def late_kernel(full, a0, a1, a2, a3, acc, out):
    store4(out, matmul4((a0, a1, a2, a3), full), acc)


def collect_kernel(s0, s1, s2, s3, full):
    assemble((s0, s1, s2, s3), full)


FULL = (2, 4, 192, 128)


def whole(shape):
    return pl.BlockSpec(shape, lambda i: (0,) * len(shape))


SHARD = whole((4, 96, 128))


def piece_specs(col):
    return [pl.BlockSpec((96, 1536), lambda i: (0, col))] * 4


def grant(mib):
    return pltpu.CompilerParams(vmem_limit_bytes=mib << 20)


COST = pl.CostEstimate(flops=2 * 384 * 1536 * 128, transcendentals=0, bytes_accessed=1600000)


def solve(shards, pieces, col):
    return pl.pallas_call(
        solve_kernel,
        grid=(1,),
        in_specs=[SHARD] * 4 + piece_specs(col),
        out_specs=(SHARD, SHARD),
        out_shape=(jax.ShapeDtypeStruct((4, 96, 128), BF), jax.ShapeDtypeStruct((4, 96, 128), F32)),
        scratch_shapes=[pltpu.VMEM(FULL, BF)],
        cost_estimate=COST,
        compiler_params=grant(6),
        name="solve",
    )(*shards, *pieces)


def update(shards, pieces, col, acc):
    return pl.pallas_call(
        update_kernel,
        grid=(1,),
        in_specs=[SHARD] * 4 + piece_specs(col) + [SHARD],
        out_specs=(SHARD, whole(FULL)),
        out_shape=(jax.ShapeDtypeStruct((4, 96, 128), BF), jax.ShapeDtypeStruct(FULL, BF)),
        cost_estimate=COST,
        compiler_params=grant(6),
        name="update",
    )(*shards, *pieces, acc)


def late(full, pieces, col, acc):
    return pl.pallas_call(
        late_kernel,
        grid=(1,),
        in_specs=[whole(FULL)] + piece_specs(col) + [SHARD],
        out_specs=SHARD,
        out_shape=jax.ShapeDtypeStruct((4, 96, 128), F32),
        cost_estimate=COST,
        compiler_params=grant(6),
        name="late",
    )(full, *pieces, acc)


def collect(shards):
    return pl.pallas_call(
        collect_kernel,
        grid=(1,),
        in_specs=[SHARD] * 4,
        out_specs=whole(FULL),
        out_shape=jax.ShapeDtypeStruct(FULL, BF),
        compiler_params=grant(4),
        name="collect",
    )(*shards)


def trail_kernel(ks, n_done, *refs):
    columns = [refs[4 * m : 4 * m + 4] for m in range(len(ks))]
    facs = refs[4 * len(ks) : 5 * len(ks)]
    acc = refs[5 * len(ks)]
    done = refs[5 * len(ks) + 1 : 5 * len(ks) + 1 + n_done]
    out, *solved = refs[5 * len(ks) + 1 + n_done :]
    y, z, c = place()

    def spot(rel):
        q = lax.rem(y + rel // 2, 2) * 2 + lax.rem(c + rel % 2, 2)
        return lanes(q * 128)

    @pl.when(pl.program_id(0) == 0)
    def _():
        rows = pl.ds(pl.multiple_of((y * 8 + z * 2 + c) * 96, 32), 96)
        for m, piece in enumerate(columns):
            for rel, ref in enumerate(piece):
                solved[m][n_done, :, spot(rel)] = ref[rows, :].astype(F32)
        for m, ref in enumerate(done):
            solved[0][m] = ref[0]

    product = None
    for piece, fac in zip(columns, facs):
        rhs = jnp.concatenate([ref[...] for ref in piece], axis=1)
        term = jnp.dot(fac[...].reshape(-1, 1536), rhs, preferred_element_type=F32)
        product = term if product is None else product + term
    product = product.reshape(-1, 96, 512)
    for rel in range(4):
        out[:, :, spot(rel)] = acc[:, :, spot(rel)] - product[:, :, rel * 128 : (rel + 1) * 128]


def pull_kernel(fac, out):
    pltpu.sync_copy(fac.at[4:16, :, 4608:6144], out)


def pull(factor):
    return pl.pallas_call(
        pull_kernel,
        in_specs=[pl.BlockSpec(memory_space=pl.ANY)],
        out_specs=pl.BlockSpec(memory_space=pltpu.VMEM),
        out_shape=jax.ShapeDtypeStruct((12, 96, 1536), BF),
        cost_estimate=pl.CostEstimate(flops=0, transcendentals=0, bytes_accessed=7000000),
        compiler_params=grant(4),
        name="pull",
    )(factor)


def trail(ks, columns, factor, acc, done=()):
    base = 1 if ks[0] == 0 else 0
    specs = [whole((1536, 128))] * (4 * len(ks))
    if factor.shape[0] == 12:
        specs += [pl.BlockSpec((4, 96, 1536), lambda i: (i, 0, 0))]
    else:
        specs += [pl.BlockSpec((4, 96, 1536), functools.partial(lambda k, i: (i + 1, 0, k), k)) for k in ks]
    specs += [pl.BlockSpec((4, 96, 512), lambda i: (i + base, 0, 0))]
    specs += [whole((1, 96, 512))] * len(done)
    rows = (len(done) + 1, 96, 512)
    shapes = [jax.ShapeDtypeStruct((12, 96, 512), F32)] + [jax.ShapeDtypeStruct(rows, F32)] * len(ks)
    return pl.pallas_call(
        functools.partial(trail_kernel, ks, len(done)),
        grid=(3,),
        in_specs=specs,
        out_specs=[pl.BlockSpec((4, 96, 512), lambda i: (i, 0, 0))] + [whole(rows)] * len(ks),
        out_shape=shapes,
        cost_estimate=pl.CostEstimate(
            flops=2 * 1152 * 1536 * 512 * len(ks), transcendentals=0, bytes_accessed=5000000 + 3500000 * len(ks)
        ),
        compiler_params=grant(18 if len(ks) > 1 else 14),
        name="trail",
    )(*[x for k in ks for x in columns[k]], *[factor] * len(ks), acc, *done)


def after(x, *values):
    return lax.optimization_barrier((x, *values))[0]


def rows_of(own):
    sib = pp(own, TO_C)
    recv = pp(own, TO_Y)
    return own, sib, recv, pp(recv, TO_C)


def swap_halves(mine):
    return lax.ppermute(mine, "col", [(i, i ^ 2) for i in range(8)])


def rows_by_halves(own, mine, other):
    sib = pp(own, TO_C)
    recv = merge(mine, other)
    return own, sib, recv, pp(recv, TO_C)


def steps(factor, inverse_blocks, right_side, shape_derivative):
    factor, inverse_hbm, right_hbm, deriv_hbm = (
        pltpu.with_memory_space_constraint(x, pltpu.HBM) for x in (factor, inverse_blocks, right_side, shape_derivative)
    )
    to_y, keep = divide(right_hbm, 0, BF)
    t = land(keep, pp(to_y, TO_Y), 1)[0]
    sets = [rows_of(inverse_blocks[0])]
    own1, to_y, keep = pack(1, False, 1, factor, inverse_hbm, right_hbm)
    sets.append(rows_of(own1))
    accs = [None, land(keep, pp(to_y, TO_Y), 1)[0], None, None]
    own2, mine2, to_y, keep2 = pack(2, True, 1, factor, inverse_hbm, right_hbm)
    mine2, from_y2 = pp(mine2, TO_Y), pp(to_y, TO_Y)
    own3, mine3, to_y, keep3 = pack(3, True, 1, factor, inverse_hbm, right_hbm)
    mine3, from_y3 = pp(mine3, TO_Y), pp(to_y, TO_Y)

    acc, solved, columns, fulls, kept = right_hbm, [], [], [], []

    def trail_step(ks, acc):
        acc, *rows = trail(ks, columns, pulled if ks[-1] == 3 else factor, acc, tuple(solved) if ks[-1] == 3 else ())
        solved.extend(rows)
        return acc

    def late_step(j, m):
        accs[j] = late(fulls[m], sets[j], m, accs[j])

    for k in range(4):
        shards = z_gather(t)
        if k == 2:
            accs[3] = land(keep3, from_y3, 1)[0]
            sets.append(rows_by_halves(own3, mine3, after(other3, t)))
            late_step(3, 0)
            late_step(3, 1)
        s, product = solve(shards, sets[k], k)
        kept.append(product)
        shards = z_gather(s)
        if k == 2:
            acc = trail_step((0,), acc)
        if k < 3:
            t, full = update(shards, sets[k + 1], k, accs[k + 1])
            fulls.append(full)
            if k == 0:
                accs[2] = land(keep2, from_y2, 1)[0]
                sets.append(rows_by_halves(own2, mine2, swap_halves(mine2)))
                late_step(2, 0)
            if k == 1:
                other3 = swap_halves(mine3)
                to_y, keep = zip(*[divide(deriv_hbm, i, F32) for i in range(4)])
                derive = pp(jnp.concatenate(to_y), TO_Y)
            if k == 2:
                deriv = land(jnp.concatenate(keep), derive, 4)
        else:
            full = collect(shards)
        s_own = full.reshape(1536, 128)
        s_y = pp(s_own, TO_Y)
        columns.append((s_own, pp(s_own, TO_C), s_y, pp(s_y, TO_C)))
    acc = trail_step((1, 2), acc)
    pulled = pull(factor)
    total = jnp.sum(jnp.stack(kept) * deriv, axis=3)
    total = total + pp(total, TO_C)
    total = total + lax.ppermute(total, "col", [(i, i ^ 1) for i in range(8)])
    for mask in (2, 6):
        total = total + lax.ppermute(total, "col", [(i, i ^ mask) for i in range(8)])
    total = total + lax.ppermute(total, ("row", "col"), [(i, i ^ 65) for i in range(128)])
    acc = trail_step((3,), acc)
    row = local_call(pick_kernel, [total], [whole((4, 4, 96))], [jax.ShapeDtypeStruct((4, 96), F32)])[0]
    return solved[-1], acc, row


def solution(mesh):
    placed = (
        P(None, "row", None),
        P(None, "row", None),
        P(None, "row", "col"),
        P(None, "row", "col"),
    )
    return jax.shard_map(
        steps,
        mesh=mesh,
        in_specs=placed,
        out_specs=(P(None, "row", "col"), P(None, "row", "col"), P(None, "row")),
        check_vma=False,
    )
```
